256 devices in a mesh: ctx: 32 (over x_lo, z, core), head: 8 (over x_hi, y).
Axes of the slice: x: 4 (x_hi: 2, x_lo: 2; x = x_hi * 2 + x_lo), y: 4, z: 8, core: 2. Of those that a mesh axis runs over, the one named last changes fastest.
Arguments:
- queries: bfloat16 [2, 8192, 32, 128], P(None, 'ctx', 'head')
- key_rows: bfloat16 [8192, 8, 128], P('ctx', 'head')
- value_rows: bfloat16 [8192, 8, 128], P('ctx', 'head'), may hold values from -6 to 6
- attn_out: bfloat16 [2, 8192, 32, 128], P(None, 'ctx', 'head'), may hold values from -3 to 3
- out_grad: bfloat16 [2, 8192, 32, 128], P(None, 'ctx', 'head'), may hold values from -6 to 6
- log_norm: float32 [2, 32, 8192], P(None, 'head', 'ctx'), as said below
- positions: int32 [8192], P('ctx'), may hold values from 0 to 8191, as said below
- key_weight: bfloat16 [8192, 8, 128], P(None, 'head'), may hold values from -0.25 to 0.25
- value_weight: bfloat16 [8192, 8, 128], P(None, 'head'), may hold values from -0.1875 to 0.1875
Outputs:
- query_grad: bfloat16 [2, 8192, 32, 128], P(None, 'ctx', 'head')
- key_grad: bfloat16 [8192, 8, 128], P('ctx', 'head')
- value_grad: bfloat16 [8192, 8, 128], P('ctx', 'head')
- input_grad: bfloat16 [8192, 8192], P('head', 'ctx')
The draws below stay inside these ranges and needn't reach their ends.
Inputs may be any that keep to these rules, and one draw needn't show every extreme that they name: positions is a permutation of the sequence's positions; the stored tokens come in runs of 128 consecutive positions in rising order, and the run of rows k * 256 to k * 256 + 256 / 2 - 1 holds run j of the sequence while the next 128 rows hold run 2 * 32 - 1 - j. log_norm is the log of the total of the softmax row that probs describes, so each row of probs sums to one.
All inputs are finite; a program needn't handle non-finite values.
Results may differ from the reference program's by a relative error of at most 0.0057.
Values may be sent and summed in bfloat16 or wider, within the bound.
No kernel may reach another device: no remote copies, remote signals or barrier semaphores. Data moves between devices by JAX's collectives and lax.ppermute only.
A program may use at most 128 MiB of HBM per device.

```python
import jax
import jax.numpy as jnp
from jax import lax

D = 8192
HD = 128
QPK = 4
LAYERS = 2
TOK_DEV = 256
KVH = 8
QH = 32
SEQ = 8192


def float_field(key, shape, factor):
    base = jax.random.truncated_normal(jax.random.fold_in(key, 1), -4.0, 4.0, shape, jnp.float32)
    return (factor * base).astype(jnp.bfloat16)


def shared_draw(key):
    half_rows = TOK_DEV // 2
    members = SEQ // TOK_DEV
    pairs = jax.random.permutation(jax.random.fold_in(key, 101), members).astype(jnp.int32)
    offsets = jnp.arange(half_rows, dtype=jnp.int32)
    early = pairs[:, None] * half_rows + offsets[None, :]
    late = (2 * members - 1 - pairs)[:, None] * half_rows + offsets[None, :]
    positions = jnp.concatenate([early, late], 1).reshape(SEQ)
    queries = float_field(jax.random.fold_in(key, 202), (LAYERS, SEQ, KVH * QPK, HD), 2.0)
    key_rows = float_field(jax.random.fold_in(key, 303), (SEQ, KVH, HD), 1.0)
    return (positions, queries, key_rows)


def draw_positions(key, part):
    return shared_draw(key)[0]


def draw_queries(key, part):
    return shared_draw(key)[1]


def draw_key_rows(key, part):
    return shared_draw(key)[2]


def draw_log_norm(key, part):
    positions, queries, key_rows = shared_draw(key)
    head_count = KVH * QPK
    query_flat = jnp.transpose(queries.astype(jnp.float32), (0, 2, 1, 3)).reshape(LAYERS * head_count, SEQ, HD)
    key_float = key_rows.astype(jnp.float32)
    allowed = positions[None, :] <= positions[:, None]

    def one_row(items):
        flat_index, query_part = items
        group_index = flat_index % head_count // QPK
        key_part = lax.dynamic_index_in_dim(key_float, group_index, 1, keepdims=False)
        scores = jnp.dot(query_part, key_part.T, precision=lax.Precision.HIGHEST) * HD ** (-0.5)
        scores = jnp.where(allowed, scores, -jnp.inf)
        return jax.nn.logsumexp(scores, axis=-1)
    totals = lax.map(one_row, (jnp.arange(LAYERS * head_count, dtype=jnp.int32), query_flat))
    return totals.reshape(LAYERS, head_count, SEQ)


def spiked(entries, key, source, target, blocks, factor):
    def block_of(axis_at):
        return (jnp.arange(entries.shape[axis_at]) // (entries.shape[axis_at] // blocks)).reshape((-1,) + (1,) * (entries.ndim - 1 - axis_at))

    one_side = jax.random.permutation(key, blocks)[block_of(target)]
    second = (block_of(target) + blocks // 2) % blocks
    return jnp.where((block_of(source) == one_side) | (block_of(source) == second), factor * entries, entries)


def level_of(stream_key, extent, cuts, least, top_value):
    factor_of, own = 1.0, jax.random.fold_in(stream_key, 6)
    for position, shards_of in cuts:
        draws = jnp.exp(jax.random.uniform(jax.random.fold_in(own, position), (shards_of,), jnp.float32, least / len(cuts), top_value / len(cuts)))
        factor_of = factor_of * jnp.repeat(draws, extent[position] // shards_of).reshape([-1 if axis == position else 1 for axis in range(len(extent))])
    return factor_of


def normal_values(rng, extent, scale, limit, cuts=(), kind=jnp.bfloat16):
    values = jax.random.normal(rng, extent, jnp.float32) * scale
    if len(cuts) > 0:
        values = level_of(rng, extent, cuts, -0.22, 0.18) * values
    return jnp.clip(values, min=-limit, max=limit).astype(kind)


def gaussian_with(own_key, extent, scale, bound, split, heavy, kind=jnp.bfloat16):
    entries = scale * jax.random.normal(own_key, extent, jnp.float32)
    if split:
        entries = entries * level_of(own_key, extent, split, -0.22, 0.18)
    return jnp.clip(spiked(entries, jax.random.fold_in(own_key, 3), *heavy), -bound, bound).astype(kind)


def setup_inputs(seed: int = 0) -> dict:
    key_of = jax.random.split(jax.random.key(seed), 10)
    queries = draw_queries(jax.random.fold_in(key_of[9], 71), 0)
    key_rows = draw_key_rows(jax.random.fold_in(key_of[9], 71), 0)
    value_rows = normal_values(key_of[2], (SEQ, KVH, HD), 1.0, 6.0, ((0, 32), (1, 8)))
    attn_out = normal_values(key_of[3], (LAYERS, SEQ, QH, HD), 0.5, 3.0, ((1, 32), (2, 8)))
    out_grad = normal_values(key_of[4], (LAYERS, SEQ, QH, HD), 1.0, 6.0, ((1, 32), (2, 8)))
    log_norm = draw_log_norm(jax.random.fold_in(key_of[9], 71), 0)
    positions = draw_positions(jax.random.fold_in(key_of[9], 71), 0)
    key_weight = gaussian_with(key_of[7], (D, KVH, HD), (KVH * HD) ** -0.5, 0.25, ((1, 8),), (1, 0, 8, 2.0))
    value_weight = normal_values(key_of[8], (D, KVH, HD), (KVH * HD) ** -0.5, 0.1875, ((1, 8),))
    return dict(queries=queries, key_rows=key_rows, value_rows=value_rows, attn_out=attn_out, out_grad=out_grad, log_norm=log_norm, positions=positions, key_weight=key_weight, value_weight=value_weight)


def rounded_half(values_in):
    return lax.optimization_barrier(values_in.astype(jnp.bfloat16)).astype(jnp.float32)


def reference(queries, key_rows, value_rows, attn_out, out_grad, log_norm, positions, key_weight, value_weight):
    layers, seq_len, head_count, head_dim = queries.shape
    kv_heads = key_rows.shape[1]
    per_group = head_count // kv_heads
    scaling = head_dim ** -0.5
    order_index = jnp.zeros((seq_len,), jnp.int32).at[positions].set(jnp.arange(seq_len, dtype=jnp.int32))
    split_shape = (layers, seq_len, kv_heads, per_group, head_dim)
    query_sorted = queries[:, order_index].astype(jnp.float32).reshape(split_shape)
    grad_sorted = out_grad[:, order_index].astype(jnp.float32).reshape(split_shape)
    deltas = jnp.sum(out_grad.astype(jnp.float32) * attn_out.astype(jnp.float32), -1)
    delta_sorted = deltas[:, order_index].reshape(layers, seq_len, kv_heads, per_group)
    norm_sorted = log_norm[:, :, order_index].reshape(layers, kv_heads, per_group, seq_len)
    keys_sorted = key_rows[order_index].astype(jnp.float32)
    values_sorted = value_rows[order_index].astype(jnp.float32)
    block = min(512, seq_len)
    highest = lax.Precision.HIGHEST
    query_parts = []
    key_total = jnp.zeros((seq_len, kv_heads, head_dim), jnp.float32)
    value_total = jnp.zeros((seq_len, kv_heads, head_dim), jnp.float32)
    for index in range(seq_len // block):
        low = index * block
        high = low + block
        allowed = jnp.arange(high)[None, :] <= jnp.arange(low, high)[:, None]
        query_heads = jnp.moveaxis(query_sorted[:, low:high], 2, 0)
        grad_heads = jnp.moveaxis(grad_sorted[:, low:high], 2, 0)
        delta_heads = jnp.moveaxis(delta_sorted[:, low:high], 2, 0)
        norm_heads = jnp.moveaxis(norm_sorted[..., low:high], 1, 0)
        key_heads = jnp.moveaxis(keys_sorted[:high], 1, 0)
        value_heads = jnp.moveaxis(values_sorted[:high], 1, 0)

        def one_head(items):
            query_part, grad_part, delta_part, norm_part, key_part, value_part = items
            scores = jnp.einsum("lrqd,kd->lqrk", query_part, key_part, precision=highest)
            shifted = jnp.where(allowed, scores * scaling - norm_part[..., None], -jnp.inf)
            probs = jnp.exp(shifted)
            dprobs = jnp.einsum("lrqd,kd->lqrk", grad_part, value_part, precision=highest)
            delta_rows = jnp.transpose(delta_part, (0, 2, 1))
            dscore = rounded_half(scaling * probs * (dprobs - delta_rows[..., None]))
            prob_half = rounded_half(probs)
            query_term = jnp.einsum("lqrk,kd->lrqd", dscore, key_part, precision=highest)
            key_term = jnp.einsum("lqrk,lrqd->kd", dscore, query_part, precision=highest)
            value_term = jnp.einsum("lqrk,lrqd->kd", prob_half, grad_part, precision=highest)
            return query_term, key_term, value_term

        query_term, key_term, value_term = lax.map(one_head, (query_heads, grad_heads, delta_heads, norm_heads, key_heads, value_heads))
        query_parts.append(jnp.moveaxis(query_term, 0, 2))
        key_total = key_total.at[:high].add(jnp.moveaxis(key_term, 0, 1))
        value_total = value_total.at[:high].add(jnp.moveaxis(value_term, 0, 1))
    query_all = jnp.concatenate(query_parts, 1)
    query_grad = query_all[:, positions].reshape(layers, seq_len, head_count, head_dim).astype(jnp.bfloat16)
    key_grad = key_total[positions].astype(jnp.bfloat16)
    value_grad = value_total[positions].astype(jnp.bfloat16)
    input_grad = jnp.einsum("cgd,tgd->ct", key_weight.astype(jnp.float32), key_grad.astype(jnp.float32), precision=highest)
    input_grad = input_grad + jnp.einsum("cgd,tgd->ct", value_weight.astype(jnp.float32), value_grad.astype(jnp.float32), precision=highest)
    return query_grad, key_grad, value_grad, input_grad.astype(jnp.bfloat16)
```

```python
import functools
import math

import jax
import jax.numpy as jnp
from jax import lax
from jax.experimental import pallas as pl
from jax.experimental.pallas import tpu as pltpu
from jax.sharding import Mesh, PartitionSpec as P

F32, BF16 = jnp.float32, jnp.bfloat16
HD = 128
RUN = 128
BLK = 2 * RUN
PAY = BLK + 16
QPK = 4
SCALING = HD**-0.5
NT = (((1,), (1,)), ((), ()))
NN = (((1,), (0,)), ((), ()))
CTX = ("xl", "z", "core")
HEAD = ("xh", "y")
COST_A = 0.05


def visits_kernel(*refs, nb, m, q_in, q_raw, kv_in, kv_raw):
    refs = list(refs)

    def take(count):
        head = refs[:count]
        del refs[:count]
        return head

    qd_hbm, aux_hbm, kv_hbm = take(nb), take(nb), take(m)
    dqi_hbm, acci_hbm = take(len(q_in)), take(2 if kv_in else 0)
    dq_hbm = take(nb)
    dkv_hbm = take(2 if kv_raw else m)
    qds, auxs, kvs, dqs, dqo, dkvo, ks, vs, kts, acck, accv = take(11)
    order, krun, qrun_s, sem, osem = take(5)
    nr = 2 * m
    layers = qds.shape[2]
    rows = qds.shape[3] // 2
    c1 = SCALING * math.log2(math.e)

    copies = [(kv_hbm[j], kvs.at[j]) for j in range(m)]
    for b in range(nb):
        copies.append((aux_hbm[b], auxs.at[b]))
        copies.append((qd_hbm[b], qds.at[b]))
    if kv_in:
        copies.append((acci_hbm[0], acck))
        copies.append((acci_hbm[1], accv))
    for i, b in enumerate(q_in):
        copies.append((dqi_hbm[i], dqs.at[b]))
    copies = [pltpu.make_async_copy(s, d, sem.at[i]) for i, (s, d) in enumerate(copies)]
    for c in copies:
        c.start()
    for b in range(nb):
        if b not in q_in:
            dqs[b] = jnp.zeros(dqs.shape[1:], F32)
    if not kv_in:
        acck[...] = jnp.zeros_like(acck)
        accv[...] = jnp.zeros_like(accv)
    for c in copies:
        c.wait()

    for j in range(m):
        for i in range(2):
            tag = kvs[j, BLK + 8 * i : BLK + 8 * i + 8, 0:HD].astype(F32)
            krun[2 * j + i] = jnp.max(tag).astype(jnp.int32)
    for b in range(nb):
        for i in range(2):
            qrun_s[2 * b + i] = jnp.max(auxs[b, 4 + i : 5 + i, 0:HD]).astype(jnp.int32)
    for i in range(nr):
        mine = krun[i]
        rank = jnp.int32(0)
        for j in range(nr):
            if j != i:
                rank = rank + (krun[j] < mine).astype(jnp.int32)
        order[rank] = i

    def arrange(i, carry):
        s = order[i]
        at = pl.multiple_of((s % 2) * RUN, RUN)
        to = pl.multiple_of(i * RUN, RUN)
        k = kvs[s // 2, pl.ds(at, RUN), 0:HD]
        ks[pl.ds(to, RUN), :] = k
        vs[pl.ds(to, RUN), :] = kvs[s // 2, pl.ds(at, RUN), HD : 2 * HD]
        kts[i // 2, i % 2] = k.T
        return carry

    lax.fori_loop(0, nr, arrange, 0)

    def query_half(qi, carry):
        b = qi // 2
        half = qi % 2
        qrun = qrun_s[qi]
        reach = jnp.int32(0)
        for j in range(nr):
            reach = reach + (krun[j] <= qrun).astype(jnp.int32)
        off = pl.multiple_of(half * rows, rows)

        def visit(p, masked):
            at = pl.multiple_of(p * BLK, BLK)
            kp = ks[pl.ds(at, BLK), :]
            vp = vs[pl.ds(at, BLK), :]
            kt = jnp.concatenate([kts[p, 0], kts[p, 1]], axis=1)
            if masked:
                first = krun[order[2 * p]] * RUN
                second = krun[order[2 * p + 1]] * RUN
                ii = lax.broadcasted_iota(jnp.int32, (BLK, 1), 0)
                kpos = jnp.where(ii < RUN, ii + first, ii - RUN + second)
                jj = lax.broadcasted_iota(jnp.int32, (1, rows), 1)
                seen = kpos <= jj // QPK + qrun * RUN
            dk = acck[p]
            dv = accv[p]
            for l in range(layers):
                q = qds[b, 0, l, pl.ds(off, rows), :]
                do = qds[b, 1, l, pl.ds(off, rows), :]
                lse = auxs[b, l : l + 1, pl.ds(off, rows)]
                delta = auxs[b, 2 + l : 3 + l, pl.ds(off, rows)]
                scores = lax.dot_general(kp, q, NT, preferred_element_type=F32)
                probs = jnp.exp2(scores * c1 - lse)
                if masked:
                    probs = jnp.where(seen, probs, 0.0)
                dprobs = lax.dot_general(vp, do, NT, preferred_element_type=F32)
                dscore = (probs * (dprobs - delta)).astype(BF16)
                dv = dv + lax.dot_general(probs.astype(BF16), do, NN, preferred_element_type=F32)
                dk = dk + lax.dot_general(dscore, q, NN, preferred_element_type=F32)
                dqs[b, half, l] += lax.dot_general(kt, dscore, NN, preferred_element_type=F32)
            acck[p] = dk
            accv[p] = dv

        def step(p, inner):
            full = krun[order[2 * p + 1]] < qrun

            @pl.when(full)
            def _():
                visit(p, False)

            @pl.when(jnp.logical_not(full))
            def _():
                visit(p, True)

            return inner

        lax.fori_loop(0, (reach + 1) // 2, step, 0)
        return carry

    lax.fori_loop(0, 2 * nb, query_half, 0)

    outs = []
    if kv_raw:
        outs += [(acck, dkv_hbm[0]), (accv, dkv_hbm[1])]
    else:

        def settle(i, carry):
            s = order[i]
            at = pl.multiple_of((i % 2) * RUN, RUN)
            to = pl.multiple_of((s % 2) * RUN, RUN)
            k_sum = acck[i // 2, pl.ds(at, RUN), :] * SCALING
            v_sum = accv[i // 2, pl.ds(at, RUN), :]
            dkvo[s // 2, pl.ds(to, RUN), 0:HD] = k_sum.astype(BF16)
            dkvo[s // 2, pl.ds(to, RUN), HD : 2 * HD] = v_sum.astype(BF16)
            return carry

        lax.fori_loop(0, nr, settle, 0)
        outs += [(dkvo.at[j], dkv_hbm[j]) for j in range(m)]
    for b in range(nb):
        if b in q_raw:
            outs.append((dqs.at[b], dq_hbm[b]))
    outs = [pltpu.make_async_copy(s, d, osem.at[i]) for i, (s, d) in enumerate(outs)]
    for c in outs:
        c.start()
    late = []
    for b in range(nb):
        if b not in q_raw:
            for half in range(2):
                for l in range(layers):
                    dqo[b, l, half * rows : (half + 1) * rows, :] = (dqs[b, half, l] * SCALING).T.astype(BF16)
            c = pltpu.make_async_copy(dqo.at[b], dq_hbm[b], osem.at[len(outs) + len(late)])
            c.start()
            late.append(c)
    for c in outs + late:
        c.wait()


def visits(name, queries, keys, q_before=None, q_raw=(), kv_before=None, kv_raw=False, cost=1.0):
    nb, m = len(queries), len(keys)
    q_before = q_before or {}
    q_in = sorted(q_before)
    _, layers, rows, _ = queries[0][0].shape
    q_shape = (layers, rows, HD)
    aux_shape = queries[0][1].shape
    operands = (
        [q[0] for q in queries]
        + [q[1] for q in queries]
        + list(keys)
        + [q_before[b] for b in q_in]
        + list(kv_before or ())
    )
    units = nb * m * 2
    any_spec = pl.BlockSpec(memory_space=pl.ANY)
    raw_shape = (2, layers, HD, rows // 2)
    acc_shape = (m, BLK, HD)
    out_shape = [
        jax.ShapeDtypeStruct(raw_shape, F32) if b in q_raw else jax.ShapeDtypeStruct(q_shape, BF16)
        for b in range(nb)
    ]
    if kv_raw:
        out_shape += [jax.ShapeDtypeStruct(acc_shape, F32)] * 2
    else:
        out_shape += [jax.ShapeDtypeStruct((BLK, 2 * HD), BF16)] * m
    outs = pl.pallas_call(
        functools.partial(
            visits_kernel,
            nb=nb,
            m=m,
            q_in=tuple(q_in),
            q_raw=tuple(q_raw),
            kv_in=kv_before is not None,
            kv_raw=kv_raw,
        ),
        out_shape=out_shape,
        in_specs=[any_spec] * len(operands),
        out_specs=[any_spec] * len(out_shape),
        scratch_shapes=[
            pltpu.VMEM((nb, 2) + q_shape, BF16),
            pltpu.VMEM((nb,) + aux_shape, F32),
            pltpu.VMEM((m, PAY, 2 * HD), BF16),
            pltpu.VMEM((nb,) + raw_shape, F32),
            pltpu.VMEM((nb, layers, rows, HD), BF16),
            pltpu.VMEM((m, BLK, 2 * HD), BF16),
            pltpu.VMEM((2 * m * RUN, HD), BF16),
            pltpu.VMEM((2 * m * RUN, HD), BF16),
            pltpu.VMEM((m, 2, HD, RUN), BF16),
            pltpu.VMEM(acc_shape, F32),
            pltpu.VMEM(acc_shape, F32),
            pltpu.SMEM((2 * m,), jnp.int32),
            pltpu.SMEM((2 * m,), jnp.int32),
            pltpu.SMEM((2 * nb,), jnp.int32),
            pltpu.SemaphoreType.DMA((len(operands),)),
            pltpu.SemaphoreType.DMA((len(out_shape),)),
        ],
        compiler_params=pltpu.CompilerParams(vmem_limit_bytes=60 * 2**20),
        cost_estimate=pl.CostEstimate(
            flops=int(cost * units * 1024 * RUN * HD * 20),
            bytes_accessed=int(cost * nb * 3 * 2**20),
            transcendentals=int(cost * units * 1024 * RUN),
        ),
        name=name,
    )(*operands)
    return outs[:nb], outs[nb:]


def tail_kernel(first_ref, second_ref, grads_ref, out_ref):
    total = jnp.zeros(out_ref.shape, F32)
    for g in range(first_ref.shape[0]):
        w = jnp.concatenate([first_ref[g], second_ref[g]], axis=1)
        total = total + lax.dot_general(w, grads_ref[g], NT, preferred_element_type=F32)
    out_ref[...] = total.astype(out_ref.dtype)


def moved(value, axis, distance):
    size = lax.axis_size(axis)
    return lax.ppermute(value, axis, [(i, (i + distance) % size) for i in range(size)])


def on_device(
    queries, key_rows, value_rows, attn_out, out_grad, log_norm, positions, key_weight, value_weight
):
    layers, tokens, per_group, head_dim = queries.shape
    rows = tokens * per_group
    zn = lax.axis_size("z")
    runs = positions.reshape(2, RUN)[:, 0] // RUN
    tags = jnp.broadcast_to(runs.astype(BF16)[:, None, None], (2, 8, 2 * head_dim)).reshape(16, 2 * head_dim)
    block = jnp.concatenate([key_rows[:, 0], value_rows[:, 0]], axis=1)
    block = jnp.concatenate([block, tags], axis=0)
    keys = {0: block}
    keys[1], keys[zn - 1] = moved(block, "z", 1), moved(block, "z", -1)
    for t in (2, 3):
        keys[t], keys[zn - t] = moved(keys[t - 1], "z", 1), moved(keys[zn - t + 1], "z", -1)
    keys[4] = moved(keys[3], "z", 1)

    q = queries.reshape(layers, rows, head_dim)
    do = out_grad.reshape(layers, rows, head_dim)
    deltas = jnp.sum(out_grad.astype(F32) * attn_out.astype(F32), -1).reshape(layers, rows)
    lse = jnp.transpose(log_norm, (0, 2, 1)).reshape(layers, rows) * math.log2(math.e)
    run_rows = jnp.broadcast_to(runs.astype(F32)[:, None], (2, rows))
    aux = jnp.concatenate([lse, deltas, run_rows, jnp.zeros((2, rows), F32)], axis=0)
    own = (jnp.stack([q, do]), aux)
    over = tuple(moved(a, "core", 1) for a in own)
    both = moved(jnp.concatenate([aux, over[1]], axis=0), "xl", 1)
    far = (moved(own[0], "xl", 1), both[:8])

    near_t = (0, 1, 2, zn - 2, zn - 1)
    far_t = (3, 4, zn - 3)
    near_k = [keys[t] for t in near_t]
    far_k = [keys[t] for t in far_t]
    dq_a, acc_a = visits("near_near", [own, over], near_k, q_raw=(0, 1), kv_raw=True, cost=COST_A)
    held, _ = lax.optimization_barrier((far[0], acc_a[0]))
    far_over = (moved(held, "core", 1), both[8:])
    dq_b, dkv_b = visits(
        "all_far",
        [own, over, far, far_over],
        far_k,
        q_before={0: dq_a[0], 1: dq_a[1]},
        q_raw=(2, 3),
    )
    core = lax.axis_index("core")
    features = key_weight.shape[0]
    kw, vw, _ = lax.optimization_barrier((key_weight[:, 0], value_weight[:, 0], dkv_b[0]))
    mine = lax.all_to_all(jnp.where(core == 0, kw, vw), HEAD, 0, 0, tiled=True)
    mine = mine.reshape(8, features // 8, head_dim)
    other = moved(mine, "core", 1)

    dq_c, dkv_c = visits(
        "far_near", [far, far_over], near_k, q_before={0: dq_b[2], 1: dq_b[3]}, kv_before=acc_a
    )
    far_total = sum(moved(part, "z", -t).astype(F32) for t, part in zip(far_t, dkv_b))
    dkv_c, far_total = lax.optimization_barrier((dkv_c, far_total))
    total = far_total + dkv_c[0].astype(F32)
    for t, part in zip(near_t[1:], dkv_c[1:]):
        total = total + moved(part, "z", -t).astype(F32)
    grads = total.astype(BF16)

    got = moved(dq_b[1], "core", 1)
    far_sum = dq_c[0].astype(F32) + moved(dq_c[1], "core", 1).astype(F32)
    got_far = moved(far_sum.astype(BF16), "xl", 1)
    query_grad = (dq_b[0].astype(F32) + got.astype(F32) + got_far.astype(F32)).astype(BF16)
    query_grad = query_grad.reshape(queries.shape)

    swapped = jnp.concatenate([grads[:, head_dim:], grads[:, :head_dim]], axis=1)
    turned = jnp.where(core == 0, grads, swapped)
    every = lax.all_to_all(
        jnp.broadcast_to(turned[None], (8,) + grads.shape), HEAD, 0, 0, tiled=True
    )
    steps = 4
    tile = features // 8 // steps
    weight_spec = pl.BlockSpec((8, tile, head_dim), lambda i: (0, i, 0))
    input_grad = pl.pallas_call(
        tail_kernel,
        grid=(steps,),
        out_shape=jax.ShapeDtypeStruct((features // 8, tokens), BF16),
        in_specs=[
            weight_spec,
            weight_spec,
            pl.BlockSpec((8, tokens, 2 * head_dim), lambda i: (0, 0, 0)),
        ],
        out_specs=pl.BlockSpec((tile, tokens), lambda i: (i, 0)),
        compiler_params=pltpu.CompilerParams(vmem_limit_bytes=60 * 2**20),
        cost_estimate=pl.CostEstimate(
            flops=2 * features * tokens * 2 * head_dim, bytes_accessed=6 * 2**20, transcendentals=0
        ),
        name="input_grad",
    )(mine, other, every)
    return (
        query_grad,
        grads[:, None, :head_dim],
        grads[:, None, head_dim:],
        input_grad,
    )


def solution(mesh):
    fine = Mesh(mesh.devices.reshape(2, 8, 2, 2, 4), CTX + HEAD)
    placed = (
        P(None, CTX, HEAD, None),
        P(CTX, HEAD, None),
        P(CTX, HEAD, None),
        P(None, CTX, HEAD, None),
        P(None, CTX, HEAD, None),
        P(None, HEAD, CTX),
        P(CTX),
        P(None, HEAD, None),
        P(None, HEAD, None),
    )
    return jax.shard_map(
        on_device,
        mesh=fine,
        in_specs=placed,
        out_specs=(
            P(None, CTX, HEAD, None),
            P(CTX, HEAD, None),
            P(CTX, HEAD, None),
            P(HEAD, CTX),
        ),
        check_vma=False,
    )
```

```python
import functools
import math

import jax
import jax.numpy as jnp
from jax import lax
from jax.experimental import pallas as pl
from jax.experimental.pallas import tpu as pltpu
from jax.sharding import Mesh, PartitionSpec as P

F32, BF16 = jnp.float32, jnp.bfloat16
HD = 128
RUN = 128
BLK = 2 * RUN
PAY = BLK + 16
QPK = 4
SCALING = HD**-0.5
NT = (((1,), (1,)), ((), ()))
NN = (((1,), (0,)), ((), ()))
CTX = ("xl", "z", "core")
HEAD = ("xh", "y")


def visits_kernel(*refs, nb, m):
    refs = list(refs)

    def take(count):
        head = refs[:count]
        del refs[:count]
        return head

    (z_ref,) = take(1)
    qd_hbm, aux_hbm, kv_hbm = take(nb), take(nb - 1), take(m)
    dq_hbm, (dkv_hbm,) = take(nb), take(1)
    qds, auxs, kvs, dqt, dqo, dkvo, ks, vs, kts, acck, accv = take(11)
    order, krun, qrun_s, sem, osem = take(5)
    nr = 2 * m
    layers = qds.shape[2]
    rows = qds.shape[3] // 2
    c1 = SCALING * math.log2(math.e)

    z = z_ref[0]
    small = [
        pltpu.make_async_copy(kv_hbm[t], kvs.at[lax.rem(z - t + m, m)], sem.at[t]) for t in range(m)
    ]
    aux_hbm = aux_hbm[: nb - 2] + [aux_hbm[-1].at[0:8], aux_hbm[-1].at[8:16]]
    small += [pltpu.make_async_copy(aux_hbm[b], auxs.at[b], sem.at[m + b]) for b in range(nb)]
    large = [pltpu.make_async_copy(qd_hbm[b], qds.at[b], sem.at[m + nb + b]) for b in range(nb)]
    for c in small + large:
        c.start()
    acck[...] = jnp.zeros_like(acck)
    accv[...] = jnp.zeros_like(accv)
    for c in small:
        c.wait()

    for j in range(m):
        for i in range(2):
            tag = kvs[j, BLK + 8 * i : BLK + 8 * i + 8, 0:HD].astype(F32)
            krun[2 * j + i] = jnp.max(tag).astype(jnp.int32)
    for b in range(nb):
        for i in range(2):
            qrun_s[2 * b + i] = jnp.max(auxs[b, 4 + i : 5 + i, 0:HD]).astype(jnp.int32)
    for i in range(nr):
        mine = krun[i]
        rank = jnp.int32(0)
        for j in range(nr):
            if j != i:
                rank = rank + (krun[j] < mine).astype(jnp.int32)
        order[rank] = i

    def arrange(i, carry):
        s = order[i]
        at = pl.multiple_of((s % 2) * RUN, RUN)
        to = pl.multiple_of(i * RUN, RUN)
        k = kvs[s // 2, pl.ds(at, RUN), 0:HD]
        ks[pl.ds(to, RUN), :] = k
        vs[pl.ds(to, RUN), :] = kvs[s // 2, pl.ds(at, RUN), HD : 2 * HD]
        kts[i // 2, i % 2] = k.T
        return carry

    lax.fori_loop(0, nr, arrange, 0)
    for c in large:
        c.wait()

    def query_half(qi, carry):
        b = qi // 2
        qrun = qrun_s[qi]
        reach = jnp.int32(0)
        for j in range(nr):
            reach = reach + (krun[j] <= qrun).astype(jnp.int32)
        off = pl.multiple_of((qi % 2) * rows, rows)
        dqt[...] = jnp.zeros_like(dqt)

        def visit(p, masked):
            at = pl.multiple_of(p * BLK, BLK)
            kp = ks[pl.ds(at, BLK), :]
            vp = vs[pl.ds(at, BLK), :]
            kt = jnp.concatenate([kts[p, 0], kts[p, 1]], axis=1)
            if masked:
                first = krun[order[2 * p]] * RUN
                second = krun[order[2 * p + 1]] * RUN
                ii = lax.broadcasted_iota(jnp.int32, (BLK, 1), 0)
                kpos = jnp.where(ii < RUN, ii + first, ii - RUN + second)
                jj = lax.broadcasted_iota(jnp.int32, (1, rows), 1)
                seen = kpos <= jj // QPK + qrun * RUN
            dk = acck[p]
            dv = accv[p]
            for l in range(layers):
                q = qds[b, 0, l, pl.ds(off, rows), :]
                do = qds[b, 1, l, pl.ds(off, rows), :]
                lse = auxs[b, l : l + 1, pl.ds(off, rows)]
                delta = auxs[b, 2 + l : 3 + l, pl.ds(off, rows)]
                scores = lax.dot_general(kp, q, NT, preferred_element_type=F32)
                probs = jnp.exp2(scores * c1 - lse)
                if masked:
                    probs = jnp.where(seen, probs, 0.0)
                dprobs = lax.dot_general(vp, do, NT, preferred_element_type=F32)
                dscore = (probs * (dprobs - delta)).astype(BF16)
                dv = dv + lax.dot_general(probs.astype(BF16), do, NN, preferred_element_type=F32)
                dk = dk + lax.dot_general(dscore, q, NN, preferred_element_type=F32)
                dqt[l] += lax.dot_general(kt, dscore, NN, preferred_element_type=F32)
            acck[p] = dk
            accv[p] = dv

        def step(p, inner):
            full = krun[order[2 * p + 1]] < qrun

            @pl.when(full)
            def _():
                visit(p, False)

            @pl.when(jnp.logical_not(full))
            def _():
                visit(p, True)

            return inner

        lax.fori_loop(0, (reach + 1) // 2, step, 0)
        for l in range(layers):
            dqo[b, l, pl.ds(off, rows), :] = (dqt[l] * SCALING).T.astype(BF16)
        return carry

    lax.fori_loop(0, 2 * nb, query_half, 0)

    def settle(i, carry):
        s = order[i]
        at = pl.multiple_of((i % 2) * RUN, RUN)
        to = pl.multiple_of((s % 2) * RUN, RUN)
        k_sum = acck[i // 2, pl.ds(at, RUN), :] * SCALING
        v_sum = accv[i // 2, pl.ds(at, RUN), :]
        dkvo[s // 2, pl.ds(to, RUN), 0:HD] = k_sum.astype(BF16)
        dkvo[s // 2, pl.ds(to, RUN), HD : 2 * HD] = v_sum.astype(BF16)
        return carry

    outs = [pltpu.make_async_copy(dqo.at[b], dq_hbm[b], osem.at[b]) for b in range(nb)]
    for c in outs:
        c.start()
    lax.fori_loop(0, nr, settle, 0)
    outs.append(pltpu.make_async_copy(dkvo, dkv_hbm, osem.at[nb]))
    outs[-1].start()
    for c in outs:
        c.wait()


def visits(z, queries, auxes, keys):
    nb, m = len(queries), len(keys)
    _, layers, rows, _ = queries[0].shape
    q_shape = (layers, rows, HD)
    aux_shape = auxes[0].shape
    operands = list(queries) + list(auxes) + list(keys)
    units = nb * m * 2
    any_spec = pl.BlockSpec(memory_space=pl.ANY)
    acc_shape = (m, BLK, HD)
    out_shape = [jax.ShapeDtypeStruct(q_shape, BF16)] * nb
    out_shape += [jax.ShapeDtypeStruct((m, BLK, 2 * HD), BF16)]
    outs = pl.pallas_call(
        functools.partial(visits_kernel, nb=nb, m=m),
        out_shape=out_shape,
        in_specs=[pl.BlockSpec(memory_space=pltpu.SMEM)] + [any_spec] * len(operands),
        out_specs=[any_spec] * len(out_shape),
        scratch_shapes=[
            pltpu.VMEM((nb, 2) + q_shape, BF16),
            pltpu.VMEM((nb,) + aux_shape, F32),
            pltpu.VMEM((m, PAY, 2 * HD), BF16),
            pltpu.VMEM((layers, HD, rows // 2), F32),
            pltpu.VMEM((nb,) + q_shape, BF16),
            pltpu.VMEM((m, BLK, 2 * HD), BF16),
            pltpu.VMEM((2 * m * RUN, HD), BF16),
            pltpu.VMEM((2 * m * RUN, HD), BF16),
            pltpu.VMEM((m, 2, HD, RUN), BF16),
            pltpu.VMEM(acc_shape, F32),
            pltpu.VMEM(acc_shape, F32),
            pltpu.SMEM((2 * m,), jnp.int32),
            pltpu.SMEM((2 * m,), jnp.int32),
            pltpu.SMEM((2 * nb,), jnp.int32),
            pltpu.SemaphoreType.DMA((m + 2 * nb,)),
            pltpu.SemaphoreType.DMA((len(out_shape),)),
        ],
        compiler_params=pltpu.CompilerParams(vmem_limit_bytes=60 * 2**20),
        cost_estimate=pl.CostEstimate(
            flops=units * 1024 * RUN * HD * 20,
            bytes_accessed=nb * 3 * 2**20,
            transcendentals=units * 1024 * RUN,
        ),
        name="visits",
    )(z.reshape(1), *operands)
    return outs


def tail_kernel(core_ref, mine_hbm, other_hbm, grads_hbm, out_ref, w, grads, sem):
    core = core_ref[0]
    heads = mine_hbm.shape[0]
    copies = []
    for g in range(heads):
        first = pl.multiple_of((2 * g + core) * HD, HD)
        second = pl.multiple_of((2 * g + 1 - core) * HD, HD)
        both = slice(2 * g * HD, 2 * (g + 1) * HD)
        copies.append(pltpu.make_async_copy(mine_hbm.at[g], w.at[:, pl.ds(first, HD)], sem.at[0, g]))
        copies.append(pltpu.make_async_copy(other_hbm.at[g], w.at[:, pl.ds(second, HD)], sem.at[1, g]))
        copies.append(pltpu.make_async_copy(grads_hbm.at[g], grads.at[:, both], sem.at[2, g]))
    for c in copies:
        c.start()
    for c in copies:
        c.wait()
    out_ref[...] = lax.dot_general(w[...], grads[...], NT, preferred_element_type=F32).astype(out_ref.dtype)


def tail(core, mine, other, grads):
    heads, features, _ = mine.shape
    tokens = grads.shape[1]
    any_spec = pl.BlockSpec(memory_space=pl.ANY)
    return pl.pallas_call(
        tail_kernel,
        out_shape=jax.ShapeDtypeStruct((features, tokens), BF16),
        in_specs=[pl.BlockSpec(memory_space=pltpu.SMEM), any_spec, any_spec, any_spec],
        out_specs=pl.BlockSpec(memory_space=pltpu.VMEM),
        scratch_shapes=[
            pltpu.VMEM((features, 2 * heads * HD), BF16),
            pltpu.VMEM((tokens, 2 * heads * HD), BF16),
            pltpu.SemaphoreType.DMA((3, heads)),
        ],
        compiler_params=pltpu.CompilerParams(vmem_limit_bytes=60 * 2**20),
        cost_estimate=pl.CostEstimate(
            flops=4 * features * tokens * heads * HD, bytes_accessed=6 * 2**20, transcendentals=0
        ),
        name="input_grad",
    )(core.reshape(1), mine, other, grads)


def moved(value, axis, distance):
    size = lax.axis_size(axis)
    return lax.ppermute(value, axis, [(i, (i + distance) % size) for i in range(size)])


def on_device(
    queries, key_rows, value_rows, attn_out, out_grad, log_norm, positions, key_weight, value_weight
):
    layers, tokens, per_group, head_dim = queries.shape
    rows = tokens * per_group
    zn = lax.axis_size("z")
    runs = positions.reshape(2, RUN)[:, 0] // RUN
    tags = jnp.broadcast_to(runs.astype(BF16)[:, None, None], (2, 8, 2 * head_dim)).reshape(16, 2 * head_dim)
    block = jnp.concatenate([key_rows[:, 0], value_rows[:, 0]], axis=1)
    block = jnp.concatenate([block, tags], axis=0)
    keys = {0: block}
    keys[1], keys[zn - 1] = moved(block, "z", 1), moved(block, "z", -1)
    for t in (2, 3):
        keys[t], keys[zn - t] = moved(keys[t - 1], "z", 1), moved(keys[zn - t + 1], "z", -1)
    keys[4] = moved(keys[3], "z", 1)

    q = queries.reshape(layers, rows, head_dim)
    do = out_grad.reshape(layers, rows, head_dim)
    deltas = jnp.sum(out_grad.astype(F32) * attn_out.astype(F32), -1).reshape(layers, rows)
    lse = jnp.transpose(log_norm, (0, 2, 1)).reshape(layers, rows) * math.log2(math.e)
    run_rows = jnp.broadcast_to(runs.astype(F32)[:, None], (2, rows))
    aux = jnp.concatenate([lse, deltas, run_rows, jnp.zeros((2, rows), F32)], axis=0)
    own = (jnp.stack([q, do]), aux)
    over = tuple(moved(a, "core", 1) for a in own)
    both = moved(jnp.concatenate([aux, over[1]], axis=0), "xl", 1)
    far = moved(own[0], "xl", 1)
    far_over = moved(far, "core", 1)

    core = lax.axis_index("core")
    features = key_weight.shape[0]
    kw, vw, _ = lax.optimization_barrier(
        (key_weight[:, 0], value_weight[:, 0], (keys[3], keys[zn - 3]))
    )
    mine = lax.all_to_all(jnp.where(core == 0, kw, vw), HEAD, 0, 0, tiled=True)
    mine = mine.reshape(8, features // 8, head_dim)
    other = moved(mine, "core", 1)

    *dq, dkv = visits(
        lax.axis_index("z"),
        [own[0], over[0], far, far_over],
        [own[1], over[1], both],
        [keys[t] for t in range(zn)],
    )
    back = lax.all_to_all(dkv, "z", 0, 0, tiled=True)
    grads = jnp.sum(back.astype(F32), axis=0).astype(BF16)

    got = moved(dq[1], "core", 1)
    far_sum = (dq[2].astype(F32) + moved(dq[3], "core", 1).astype(F32)).astype(BF16)
    got_far = moved(far_sum, "xl", 1)
    grads, got_far, got = lax.optimization_barrier((grads, got_far, got))
    query_grad = (dq[0].astype(F32) + got.astype(F32) + got_far.astype(F32)).astype(BF16)
    query_grad = query_grad.reshape(queries.shape)

    every = lax.all_to_all(
        jnp.broadcast_to(grads[None], (8,) + grads.shape), HEAD, 0, 0, tiled=True
    )
    input_grad = tail(core, mine, other, every)
    return (
        query_grad,
        grads[:, None, :head_dim],
        grads[:, None, head_dim:],
        input_grad,
    )


def solution(mesh):
    fine = Mesh(mesh.devices.reshape(2, 8, 2, 2, 4), CTX + HEAD)
    placed = (
        P(None, CTX, HEAD, None),
        P(CTX, HEAD, None),
        P(CTX, HEAD, None),
        P(None, CTX, HEAD, None),
        P(None, CTX, HEAD, None),
        P(None, HEAD, CTX),
        P(CTX),
        P(None, HEAD, None),
        P(None, HEAD, None),
    )
    return jax.shard_map(
        on_device,
        mesh=fine,
        in_specs=placed,
        out_specs=(
            P(None, CTX, HEAD, None),
            P(CTX, HEAD, None),
            P(CTX, HEAD, None),
            P(HEAD, CTX),
        ),
        check_vma=False,
    )
```

```python
import functools
import math

import jax
import jax.numpy as jnp
from jax import lax
from jax.experimental import pallas as pl
from jax.experimental.pallas import tpu as pltpu
from jax.sharding import Mesh, PartitionSpec as P

F32, BF16 = jnp.float32, jnp.bfloat16
HD = 128
RUN = 128
BLK = 2 * RUN
PAY = BLK + 16
QPK = 4
WIDE = 4
SCALING = HD**-0.5
NT = (((1,), (1,)), ((), ()))
NN = (((1,), (0,)), ((), ()))
CTX = ("xl", "z", "core")
HEAD = ("xh", "y")


def visits_kernel(*refs, nb, m):
    refs = list(refs)

    def take(count):
        head = refs[:count]
        del refs[:count]
        return head

    (z_ref,) = take(1)
    qd_hbm, aux_hbm, kv_hbm = take(nb), take(nb - 1), take(m)
    dq_hbm, (dkv_hbm,) = take(nb), take(1)
    qds, auxs, kvs, dqt, dqo, dkvo, ks, vs, kts, acck, accv = take(11)
    order, krun, qrun_s, sem, osem = take(5)
    nr = 2 * m
    layers = qds.shape[2]
    rows = qds.shape[3] // 2
    c1 = SCALING * math.log2(math.e)

    z = z_ref[0]
    small = [
        pltpu.make_async_copy(kv_hbm[t], kvs.at[lax.rem(z - t + m, m)], sem.at[t]) for t in range(m)
    ]
    aux_hbm = aux_hbm[: nb - 2] + [aux_hbm[-1].at[0:8], aux_hbm[-1].at[8:16]]
    small += [pltpu.make_async_copy(aux_hbm[b], auxs.at[b], sem.at[m + b]) for b in range(nb)]
    large = [pltpu.make_async_copy(qd_hbm[b], qds.at[b], sem.at[m + nb + b]) for b in range(nb)]
    for c in small + large:
        c.start()
    acck[...] = jnp.zeros_like(acck)
    accv[...] = jnp.zeros_like(accv)
    for c in small:
        c.wait()

    for j in range(m):
        for i in range(2):
            tag = kvs[j, BLK + 8 * i : BLK + 8 * i + 8, 0:HD].astype(F32)
            krun[2 * j + i] = jnp.max(tag).astype(jnp.int32)
    for b in range(nb):
        for i in range(2):
            qrun_s[2 * b + i] = jnp.max(auxs[b, 4 + i : 5 + i, 0:HD]).astype(jnp.int32)
    held = [krun[j] for j in range(nr)]
    for i in range(nr):
        rank = jnp.int32(0)
        for j in range(nr):
            if j != i:
                rank = rank + (held[j] < held[i]).astype(jnp.int32)
        order[rank] = i

    def arrange(i, carry):
        s = order[i]
        at = pl.multiple_of((s % 2) * RUN, RUN)
        to = pl.multiple_of(i * RUN, RUN)
        k = kvs[s // 2, pl.ds(at, RUN), 0:HD]
        ks[pl.ds(to, RUN), :] = k
        vs[pl.ds(to, RUN), :] = kvs[s // 2, pl.ds(at, RUN), HD : 2 * HD]
        kts[i // 2, i % 2] = k.T
        return carry

    lax.fori_loop(0, nr, arrange, 0)
    outs = [pltpu.make_async_copy(dqo.at[b], dq_hbm[b], osem.at[b]) for b in range(nb)]

    def query_half(qi, carry):
        b = qi // 2
        for i in range(nb):

            @pl.when(qi == 2 * i)
            def _():
                large[i].wait()

        qrun = qrun_s[qi]
        reach = jnp.int32(0)
        before = jnp.int32(0)
        for j in range(nr):
            reach = reach + (krun[j] <= qrun).astype(jnp.int32)
            before = before + (krun[j] < qrun).astype(jnp.int32)
        off = pl.multiple_of((qi % 2) * rows, rows)
        dqt[...] = jnp.zeros_like(dqt)

        def visit(p, masked, runs=2):
            keys = pl.ds(pl.multiple_of(p * BLK, BLK), runs * RUN)
            kp = ks[keys, :]
            vp = vs[keys, :]
            kt = jnp.concatenate([kts[p + i // 2, i % 2] for i in range(runs)], axis=1)
            if masked:
                first = krun[order[2 * p]] * RUN
                second = krun[order[2 * p + 1]] * RUN
                ii = lax.broadcasted_iota(jnp.int32, (BLK, 1), 0)
                kpos = jnp.where(ii < RUN, ii + first, ii - RUN + second)
                jj = lax.broadcasted_iota(jnp.int32, (1, rows), 1)
                seen = kpos <= jj // QPK + qrun * RUN
            dk = acck[keys, :]
            dv = accv[keys, :]
            for l in range(layers):
                q = qds[b, 0, l, pl.ds(off, rows), :]
                do = qds[b, 1, l, pl.ds(off, rows), :]
                lse = auxs[b, l : l + 1, pl.ds(off, rows)]
                delta = auxs[b, 2 + l : 3 + l, pl.ds(off, rows)]
                scores = lax.dot_general(kp, q, NT, preferred_element_type=F32)
                probs = jnp.exp2(scores * c1 - lse)
                if masked:
                    probs = jnp.where(seen, probs, 0.0)
                dprobs = lax.dot_general(vp, do, NT, preferred_element_type=F32)
                dscore = ((probs * SCALING) * (dprobs - delta)).astype(BF16)
                dv = dv + lax.dot_general(probs.astype(BF16), do, NN, preferred_element_type=F32)
                dk = dk + lax.dot_general(dscore, q, NN, preferred_element_type=F32)
                dqt[l] += lax.dot_general(kt, dscore, NN, preferred_element_type=F32)
            acck[keys, :] = dk
            accv[keys, :] = dv

        def step(p, inner):
            full = krun[order[2 * p + 1]] < qrun

            @pl.when(full)
            def _():
                visit(p, False)

            @pl.when(jnp.logical_not(full))
            def _():
                visit(p, True)

            return inner

        def wide_step(p, inner):
            visit(p * (WIDE // 2), False, WIDE)
            return inner

        wide = before // WIDE
        lax.fori_loop(0, wide, wide_step, 0)
        lax.fori_loop(wide * (WIDE // 2), (reach + 1) // 2, step, 0)
        for l in range(layers):
            dqo[b, l, pl.ds(off, rows), :] = dqt[l].T.astype(BF16)
        for i in range(nb):

            @pl.when(qi == 2 * i + 1)
            def _():
                outs[i].start()

        return carry

    lax.fori_loop(0, 2 * nb, query_half, 0)

    def settle(i, carry):
        s = order[i]
        at = pl.multiple_of(i * RUN, RUN)
        to = pl.multiple_of((s % 2) * RUN, RUN)
        k_sum = acck[pl.ds(at, RUN), :]
        v_sum = accv[pl.ds(at, RUN), :]
        dkvo[s // 2, pl.ds(to, RUN), 0:HD] = k_sum.astype(BF16)
        dkvo[s // 2, pl.ds(to, RUN), HD : 2 * HD] = v_sum.astype(BF16)
        return carry

    lax.fori_loop(0, nr, settle, 0)
    outs.append(pltpu.make_async_copy(dkvo, dkv_hbm, osem.at[nb]))
    outs[-1].start()
    for c in outs:
        c.wait()


def visits(z, queries, auxes, keys):
    nb, m = len(queries), len(keys)
    _, layers, rows, _ = queries[0].shape
    q_shape = (layers, rows, HD)
    aux_shape = auxes[0].shape
    operands = list(queries) + list(auxes) + list(keys)
    units = nb * m * 2
    any_spec = pl.BlockSpec(memory_space=pl.ANY)
    acc_shape = (m * BLK, HD)
    out_shape = [jax.ShapeDtypeStruct(q_shape, BF16)] * nb
    out_shape += [jax.ShapeDtypeStruct((m, BLK, 2 * HD), BF16)]
    outs = pl.pallas_call(
        functools.partial(visits_kernel, nb=nb, m=m),
        out_shape=out_shape,
        in_specs=[pl.BlockSpec(memory_space=pltpu.SMEM)] + [any_spec] * len(operands),
        out_specs=[any_spec] * len(out_shape),
        scratch_shapes=[
            pltpu.VMEM((nb, 2) + q_shape, BF16),
            pltpu.VMEM((nb,) + aux_shape, F32),
            pltpu.VMEM((m, PAY, 2 * HD), BF16),
            pltpu.VMEM((layers, HD, rows // 2), F32),
            pltpu.VMEM((nb,) + q_shape, BF16),
            pltpu.VMEM((m, BLK, 2 * HD), BF16),
            pltpu.VMEM((2 * m * RUN, HD), BF16),
            pltpu.VMEM((2 * m * RUN, HD), BF16),
            pltpu.VMEM((m, 2, HD, RUN), BF16),
            pltpu.VMEM(acc_shape, F32),
            pltpu.VMEM(acc_shape, F32),
            pltpu.SMEM((2 * m,), jnp.int32),
            pltpu.SMEM((2 * m,), jnp.int32),
            pltpu.SMEM((2 * nb,), jnp.int32),
            pltpu.SemaphoreType.DMA((m + 2 * nb,)),
            pltpu.SemaphoreType.DMA((len(out_shape),)),
        ],
        compiler_params=pltpu.CompilerParams(vmem_limit_bytes=60 * 2**20),
        cost_estimate=pl.CostEstimate(
            flops=units * 1024 * RUN * HD * 20,
            bytes_accessed=nb * 3 * 2**20,
            transcendentals=units * 1024 * RUN,
        ),
        name="visits",
    )(z.reshape(1), *operands)
    return outs


def tail_kernel(core_ref, mine_ref, other_ref, grads_ref, out_ref):
    first = core_ref[0] == 0
    total = jnp.zeros(out_ref.shape, F32)
    for g in range(mine_ref.shape[0]):
        w = jnp.concatenate([mine_ref[g], other_ref[g]], axis=1)
        key, value = grads_ref[g, :, :HD], grads_ref[g, :, HD:]
        mine, other = jnp.where(first, key, value), jnp.where(first, value, key)
        grads = jnp.concatenate([mine, other], axis=1)
        total = total + lax.dot_general(w, grads, NT, preferred_element_type=F32)
    out_ref[...] = total.astype(out_ref.dtype)


def tail(core, mine, other, grads):
    heads, features, _ = mine.shape
    tokens = grads.shape[1]
    vm = pl.BlockSpec(memory_space=pltpu.VMEM)
    return pl.pallas_call(
        tail_kernel,
        out_shape=jax.ShapeDtypeStruct((features, tokens), BF16),
        in_specs=[pl.BlockSpec(memory_space=pltpu.SMEM), vm, vm, vm],
        out_specs=vm,
        compiler_params=pltpu.CompilerParams(vmem_limit_bytes=24 * 2**20),
        cost_estimate=pl.CostEstimate(
            flops=4 * features * tokens * heads * HD, bytes_accessed=6 * 2**20, transcendentals=0
        ),
        name="input_grad",
    )(core.reshape(1), mine, other, grads)


def moved(value, axis, distance):
    size = lax.axis_size(axis)
    return lax.ppermute(value, axis, [(i, (i + distance) % size) for i in range(size)])


def on_device(
    queries, key_rows, value_rows, attn_out, out_grad, log_norm, positions, key_weight, value_weight
):
    layers, tokens, per_group, head_dim = queries.shape
    rows = tokens * per_group
    zn = lax.axis_size("z")
    runs = positions.reshape(2, RUN)[:, 0] // RUN
    tags = jnp.broadcast_to(runs.astype(BF16)[:, None, None], (2, 8, 2 * head_dim)).reshape(16, 2 * head_dim)
    block = jnp.concatenate([key_rows[:, 0], value_rows[:, 0]], axis=1)
    block = jnp.concatenate([block, tags], axis=0)
    keys = {0: block}
    keys[1], keys[zn - 1] = moved(block, "z", 1), moved(block, "z", -1)
    for t in (2, 3):
        keys[t], keys[zn - t] = moved(keys[t - 1], "z", 1), moved(keys[zn - t + 1], "z", -1)
    keys[4] = moved(keys[3], "z", 1)

    q = queries.reshape(layers, rows, head_dim)
    do = out_grad.reshape(layers, rows, head_dim)
    deltas = jnp.sum(out_grad.astype(F32) * attn_out.astype(F32), -1).reshape(layers, rows)
    lse = jnp.transpose(log_norm, (0, 2, 1)).reshape(layers, rows) * math.log2(math.e)
    run_rows = jnp.broadcast_to(runs.astype(F32)[:, None], (2, rows))
    aux = jnp.concatenate([lse, deltas, run_rows, jnp.zeros((2, rows), F32)], axis=0)
    own = (jnp.stack([q, do]), aux)
    over = tuple(moved(a, "core", 1) for a in own)
    both = moved(jnp.concatenate([aux, over[1]], axis=0), "xl", 1)
    far = moved(own[0], "xl", 1)
    far_over = moved(far, "core", 1)

    core = lax.axis_index("core")
    features = key_weight.shape[0]
    kw, vw, _ = lax.optimization_barrier(
        (key_weight[:, 0], value_weight[:, 0], (keys[3], keys[zn - 3]))
    )
    mine = lax.all_to_all(jnp.where(core == 0, kw, vw), HEAD, 0, 0, tiled=True)
    mine = mine.reshape(8, features // 8, head_dim)
    other = moved(mine, "core", 1)

    *dq, dkv = visits(
        lax.axis_index("z"),
        [own[0], over[0], far, far_over],
        [own[1], over[1], both],
        [keys[t] for t in range(zn)],
    )
    back = lax.all_to_all(dkv, "z", 0, 0, tiled=True)
    grads = jnp.sum(back.astype(F32), axis=0).astype(BF16)

    got = moved(dq[1], "core", 1)
    far_sum = (dq[2].astype(F32) + moved(dq[3], "core", 1).astype(F32)).astype(BF16)
    got_far = moved(far_sum, "xl", 1)
    grads, got_far, got = lax.optimization_barrier((grads, got_far, got))
    query_grad = (dq[0].astype(F32) + got.astype(F32) + got_far.astype(F32)).astype(BF16)
    query_grad = query_grad.reshape(queries.shape)

    every = lax.all_to_all(
        jnp.broadcast_to(grads[None], (8,) + grads.shape), HEAD, 0, 0, tiled=True
    )
    input_grad = tail(core, mine, other, every)
    return (
        query_grad,
        grads[:, None, :head_dim],
        grads[:, None, head_dim:],
        input_grad,
    )


def solution(mesh):
    fine = Mesh(mesh.devices.reshape(2, 8, 2, 2, 4), CTX + HEAD)
    placed = (
        P(None, CTX, HEAD, None),
        P(CTX, HEAD, None),
        P(CTX, HEAD, None),
        P(None, CTX, HEAD, None),
        P(None, CTX, HEAD, None),
        P(None, HEAD, CTX),
        P(CTX),
        P(None, HEAD, None),
        P(None, HEAD, None),
    )
    return jax.shard_map(
        on_device,
        mesh=fine,
        in_specs=placed,
        out_specs=(
            P(None, CTX, HEAD, None),
            P(CTX, HEAD, None),
            P(CTX, HEAD, None),
            P(HEAD, CTX),
        ),
        check_vma=False,
    )
```

```python
import functools
import math

import jax
import jax.numpy as jnp
from jax import lax
from jax.experimental import pallas as pl
from jax.experimental.pallas import tpu as pltpu
from jax.sharding import Mesh, PartitionSpec as P

F32, BF16 = jnp.float32, jnp.bfloat16
HD = 128
RUN = 128
BLK = 2 * RUN
PAY = BLK + 16
QPK = 4
WIDE = 4
SCALING = HD**-0.5
NT = (((1,), (1,)), ((), ()))
NN = (((1,), (0,)), ((), ()))
CTX = ("xl", "z", "core")
HEAD = ("xh", "y")


def visits_kernel(*refs, nb, m):
    refs = list(refs)

    def take(count):
        head = refs[:count]
        del refs[:count]
        return head

    (z_ref,) = take(1)
    qd_hbm, aux_hbm, kv_hbm = take(nb), take(nb - 1), take(m)
    dq_hbm, (dkv_hbm,) = take(nb), take(1)
    qds, auxs, kvs, dqt, dqo, dkvo, ks, vs, kts, acck, accv = take(11)
    order, krun, qrun_s, sem, osem = take(5)
    nr = 2 * m
    layers = qds.shape[2]
    rows = qds.shape[3] // 2
    c1 = SCALING * math.log2(math.e)

    z = z_ref[0]
    small = [
        pltpu.make_async_copy(kv_hbm[t], kvs.at[lax.rem(z - t + m, m)], sem.at[t]) for t in range(m)
    ]
    aux_hbm = aux_hbm[: nb - 2] + [aux_hbm[-1].at[0:8], aux_hbm[-1].at[8:16]]
    small += [pltpu.make_async_copy(aux_hbm[b], auxs.at[b], sem.at[m + b]) for b in range(nb)]
    large = [pltpu.make_async_copy(qd_hbm[b], qds.at[b], sem.at[m + nb + b]) for b in range(nb)]
    for c in small + large:
        c.start()
    acck[...] = jnp.zeros_like(acck)
    accv[...] = jnp.zeros_like(accv)
    for c in small:
        c.wait()

    for j in range(m):
        for i in range(2):
            tag = kvs[j, BLK + 8 * i : BLK + 8 * i + 8, 0:HD].astype(F32)
            krun[2 * j + i] = jnp.max(tag).astype(jnp.int32)
    for b in range(nb):
        for i in range(2):
            qrun_s[2 * b + i] = jnp.max(auxs[b, 4 + i : 5 + i, 0:HD]).astype(jnp.int32)
    held = [krun[j] for j in range(nr)]
    for i in range(nr):
        rank = jnp.int32(0)
        for j in range(nr):
            if j != i:
                rank = rank + (held[j] < held[i]).astype(jnp.int32)
        order[rank] = i

    def arrange(i, carry):
        s = order[i]
        at = pl.multiple_of((s % 2) * RUN, RUN)
        to = pl.multiple_of(i * RUN, RUN)
        k = kvs[s // 2, pl.ds(at, RUN), 0:HD]
        ks[pl.ds(to, RUN), :] = k
        vs[pl.ds(to, RUN), :] = kvs[s // 2, pl.ds(at, RUN), HD : 2 * HD]
        kts[i // 2, i % 2] = k.T
        return carry

    lax.fori_loop(0, nr, arrange, 0)
    outs = [pltpu.make_async_copy(dqo.at[b], dq_hbm[b], osem.at[b]) for b in range(nb)]

    def query_half(qi, carry):
        b = qi // 2
        for i in range(nb):

            @pl.when(qi == 2 * i)
            def _():
                large[i].wait()

        qrun = qrun_s[qi]
        reach = jnp.int32(0)
        before = jnp.int32(0)
        for j in range(nr):
            reach = reach + (krun[j] <= qrun).astype(jnp.int32)
            before = before + (krun[j] < qrun).astype(jnp.int32)
        off = pl.multiple_of((qi % 2) * rows, rows)
        dqt[...] = jnp.zeros_like(dqt)

        def visit(p, masked, runs=2):
            keys = pl.ds(pl.multiple_of(p * BLK, BLK), runs * RUN)
            kp = ks[keys, :]
            vp = vs[keys, :]
            kt = jnp.concatenate([kts[p + i // 2, i % 2] for i in range(runs)], axis=1)
            if masked:
                first = krun[order[2 * p]] * RUN
                second = krun[order[2 * p + 1]] * RUN
                ii = lax.broadcasted_iota(jnp.int32, (BLK, 1), 0)
                kpos = jnp.where(ii < RUN, ii + first, ii - RUN + second)
                jj = lax.broadcasted_iota(jnp.int32, (1, rows), 1)
                seen = kpos <= jj // QPK + qrun * RUN
            dk = acck[keys, :]
            dv = accv[keys, :]
            for l in range(layers):
                q = qds[b, 0, l, pl.ds(off, rows), :]
                do = qds[b, 1, l, pl.ds(off, rows), :]
                lse = auxs[b, l : l + 1, pl.ds(off, rows)]
                delta = auxs[b, 2 + l : 3 + l, pl.ds(off, rows)]
                scores = lax.dot_general(kp, q, NT, preferred_element_type=F32)
                probs = jnp.exp2(scores * c1 - lse)
                if masked:
                    probs = jnp.where(seen, probs, 0.0)
                dprobs = lax.dot_general(vp, do, NT, preferred_element_type=F32)
                dscore = ((probs * SCALING) * (dprobs - delta)).astype(BF16)
                dv = dv + lax.dot_general(probs.astype(BF16), do, NN, preferred_element_type=F32)
                dk = dk + lax.dot_general(dscore, q, NN, preferred_element_type=F32)
                dqt[l] += lax.dot_general(kt, dscore, NN, preferred_element_type=F32)
            acck[keys, :] = dk
            accv[keys, :] = dv

        def step(p, inner):
            full = krun[order[2 * p + 1]] < qrun

            @pl.when(full)
            def _():
                visit(p, False)

            @pl.when(jnp.logical_not(full))
            def _():
                visit(p, True)

            return inner

        def wide_step(p, inner):
            visit(p * (WIDE // 2), False, WIDE)
            return inner

        wide = before // WIDE
        lax.fori_loop(0, wide, wide_step, 0)
        lax.fori_loop(wide * (WIDE // 2), (reach + 1) // 2, step, 0)
        for l in range(layers):
            dqo[b, l, pl.ds(off, rows), :] = dqt[l].T.astype(BF16)
        for i in range(nb):

            @pl.when(qi == 2 * i + 1)
            def _():
                outs[i].start()

        return carry

    lax.fori_loop(0, 2 * nb, query_half, 0)

    def settle(i, carry):
        s = order[i]
        at = pl.multiple_of(i * RUN, RUN)
        to = pl.multiple_of((s % 2) * RUN, RUN)
        k_sum = acck[pl.ds(at, RUN), :]
        v_sum = accv[pl.ds(at, RUN), :]
        dkvo[s // 2, pl.ds(to, RUN), 0:HD] = k_sum.astype(BF16)
        dkvo[s // 2, pl.ds(to, RUN), HD : 2 * HD] = v_sum.astype(BF16)
        return carry

    lax.fori_loop(0, nr, settle, 0)
    outs.append(pltpu.make_async_copy(dkvo, dkv_hbm, osem.at[nb]))
    outs[-1].start()
    for c in outs:
        c.wait()


def visits(z, queries, auxes, keys):
    nb, m = len(queries), len(keys)
    _, layers, rows, _ = queries[0].shape
    q_shape = (layers, rows, HD)
    aux_shape = auxes[0].shape
    operands = list(queries) + list(auxes) + list(keys)
    units = nb * m * 2
    any_spec = pl.BlockSpec(memory_space=pl.ANY)
    acc_shape = (m * BLK, HD)
    out_shape = [jax.ShapeDtypeStruct(q_shape, BF16)] * nb
    out_shape += [jax.ShapeDtypeStruct((m, BLK, 2 * HD), BF16)]
    outs = pl.pallas_call(
        functools.partial(visits_kernel, nb=nb, m=m),
        out_shape=out_shape,
        in_specs=[pl.BlockSpec(memory_space=pltpu.SMEM)] + [any_spec] * len(operands),
        out_specs=[any_spec] * len(out_shape),
        scratch_shapes=[
            pltpu.VMEM((nb, 2) + q_shape, BF16),
            pltpu.VMEM((nb,) + aux_shape, F32),
            pltpu.VMEM((m, PAY, 2 * HD), BF16),
            pltpu.VMEM((layers, HD, rows // 2), F32),
            pltpu.VMEM((nb,) + q_shape, BF16),
            pltpu.VMEM((m, BLK, 2 * HD), BF16),
            pltpu.VMEM((2 * m * RUN, HD), BF16),
            pltpu.VMEM((2 * m * RUN, HD), BF16),
            pltpu.VMEM((m, 2, HD, RUN), BF16),
            pltpu.VMEM(acc_shape, F32),
            pltpu.VMEM(acc_shape, F32),
            pltpu.SMEM((2 * m,), jnp.int32),
            pltpu.SMEM((2 * m,), jnp.int32),
            pltpu.SMEM((2 * nb,), jnp.int32),
            pltpu.SemaphoreType.DMA((m + 2 * nb,)),
            pltpu.SemaphoreType.DMA((len(out_shape),)),
        ],
        compiler_params=pltpu.CompilerParams(vmem_limit_bytes=60 * 2**20),
        cost_estimate=pl.CostEstimate(
            flops=units * 1024 * RUN * HD * 20,
            bytes_accessed=nb * 3 * 2**20,
            transcendentals=units * 1024 * RUN,
        ),
        name="visits",
    )(z.reshape(1), *operands)
    return outs


def tail_kernel(core_ref, mine_ref, other_ref, grads_ref, out_ref):
    first = core_ref[0] == 0
    total = jnp.zeros(out_ref.shape, F32)
    for g in range(mine_ref.shape[0]):
        w = jnp.concatenate([mine_ref[g], other_ref[g]], axis=1)
        key, value = grads_ref[g, :, :HD], grads_ref[g, :, HD:]
        mine, other = jnp.where(first, key, value), jnp.where(first, value, key)
        grads = jnp.concatenate([mine, other], axis=1)
        total = total + lax.dot_general(w, grads, NT, preferred_element_type=F32)
    out_ref[...] = total.astype(out_ref.dtype)


def tail(core, mine, other, grads):
    heads, features, _ = mine.shape
    tokens = grads.shape[1]
    vm = pl.BlockSpec(memory_space=pltpu.VMEM)
    return pl.pallas_call(
        tail_kernel,
        out_shape=jax.ShapeDtypeStruct((features, tokens), BF16),
        in_specs=[pl.BlockSpec(memory_space=pltpu.SMEM), vm, vm, vm],
        out_specs=vm,
        compiler_params=pltpu.CompilerParams(vmem_limit_bytes=24 * 2**20),
        cost_estimate=pl.CostEstimate(
            flops=4 * features * tokens * heads * HD, bytes_accessed=6 * 2**20, transcendentals=0
        ),
        name="input_grad",
    )(core.reshape(1), mine, other, grads)


def moved(value, axis, distance):
    size = lax.axis_size(axis)
    return lax.ppermute(value, axis, [(i, (i + distance) % size) for i in range(size)])


def on_device(
    queries, key_rows, value_rows, attn_out, out_grad, log_norm, positions, key_weight, value_weight
):
    layers, tokens, per_group, head_dim = queries.shape
    rows = tokens * per_group
    zn = lax.axis_size("z")
    runs = positions.reshape(2, RUN)[:, 0] // RUN
    tags = jnp.broadcast_to(runs.astype(BF16)[:, None, None], (2, 8, 2 * head_dim)).reshape(16, 2 * head_dim)
    block = jnp.concatenate([key_rows[:, 0], value_rows[:, 0]], axis=1)
    block = jnp.concatenate([block, tags], axis=0)
    keys = {0: block}
    keys[1], keys[zn - 1] = moved(block, "z", 1), moved(block, "z", -1)
    for t in (2, 3):
        keys[t], keys[zn - t] = moved(keys[t - 1], "z", 1), moved(keys[zn - t + 1], "z", -1)
    keys[4] = moved(keys[3], "z", 1)

    q = queries.reshape(layers, rows, head_dim)
    do = out_grad.reshape(layers, rows, head_dim)
    deltas = jnp.sum(out_grad.astype(F32) * attn_out.astype(F32), -1).reshape(layers, rows)
    lse = jnp.transpose(log_norm, (0, 2, 1)).reshape(layers, rows) * math.log2(math.e)
    run_rows = jnp.broadcast_to(runs.astype(F32)[:, None], (2, rows))
    aux = jnp.concatenate([lse, deltas, run_rows, jnp.zeros((2, rows), F32)], axis=0)
    own = (jnp.stack([q, do]), aux)
    over = tuple(moved(a, "core", 1) for a in own)
    both = moved(jnp.concatenate([aux, over[1]], axis=0), "xl", 1)
    far = moved(own[0], "xl", 1)
    far_over = moved(far, "core", 1)

    core = lax.axis_index("core")
    features = key_weight.shape[0]
    picked = jnp.where(core == 0, key_weight[:, 0], value_weight[:, 0])
    picked, third, third_back = lax.optimization_barrier(
        (picked, keys[3], keys[zn - 3])
    )
    keys[3], keys[zn - 3] = third, third_back
    mine = lax.all_to_all(picked, HEAD, 0, 0, tiled=True)
    mine = mine.reshape(8, features // 8, head_dim)
    other = moved(mine, "core", 1)

    *dq, dkv = visits(
        lax.axis_index("z"),
        [own[0], over[0], far, far_over],
        [own[1], over[1], both],
        [keys[t] for t in range(zn)],
    )
    back = lax.all_to_all(dkv, "z", 0, 0, tiled=True)
    grads = jnp.sum(back.astype(F32), axis=0).astype(BF16)

    got = moved(dq[1], "core", 1)
    far_sum = (dq[2].astype(F32) + moved(dq[3], "core", 1).astype(F32)).astype(BF16)
    got_far = moved(far_sum, "xl", 1)
    grads, got_far, got = lax.optimization_barrier((grads, got_far, got))
    query_grad = (dq[0].astype(F32) + got.astype(F32) + got_far.astype(F32)).astype(BF16)
    query_grad = query_grad.reshape(queries.shape)

    every = lax.all_to_all(
        jnp.broadcast_to(grads[None], (8,) + grads.shape), HEAD, 0, 0, tiled=True
    )
    input_grad = tail(core, mine, other, every)
    return (
        query_grad,
        grads[:, None, :head_dim],
        grads[:, None, head_dim:],
        input_grad,
    )


def solution(mesh):
    fine = Mesh(mesh.devices.reshape(2, 8, 2, 2, 4), CTX + HEAD)
    placed = (
        P(None, CTX, HEAD, None),
        P(CTX, HEAD, None),
        P(CTX, HEAD, None),
        P(None, CTX, HEAD, None),
        P(None, CTX, HEAD, None),
        P(None, HEAD, CTX),
        P(CTX),
        P(None, HEAD, None),
        P(None, HEAD, None),
    )
    return jax.shard_map(
        on_device,
        mesh=fine,
        in_specs=placed,
        out_specs=(
            P(None, CTX, HEAD, None),
            P(CTX, HEAD, None),
            P(CTX, HEAD, None),
            P(HEAD, CTX),
        ),
        check_vma=False,
    )
```
